32 devices in a mesh: day: 2 (over core), region: 4 (over y, x), scen: 4 (over z).
Axes of the slice: x: 2, y: 2, z: 4, core: 2. Of those that a mesh axis runs over, the one named last changes fastest.
Arguments:
- shipments_init: float32 [4, 4, 4, 128, 2, 256], P('scen', 'region', None, None, 'day'), may hold values from 0 to 1
- holdings_init: float32 [4, 400, 2, 6, 256], P('scen', 'region', 'day'), may hold values from 0 to 2
- selling_init: float32 [4, 400, 2, 6, 256], P('scen', 'region', 'day'), may hold values from 0 to 1
- shortage_init: float32 [4, 400, 2, 256], P('scen', 'region', 'day'), may hold values from 0 to 1
- ordering_init: float32 [60, 256], P('region'), may hold values from 0 to 20
- balance_dual_init: float32 [4, 400, 2, 6, 256], P('scen', 'region', 'day'), may hold values from -3 to 3
- demand_dual_init: float32 [4, 400, 2, 256], P('scen', 'region', 'day'), may hold values from -3 to 3
- depot_dual_init: float32 [4, 60, 2, 256], P('scen', 'region', 'day'), may hold values from 0 to 0.1
- demand_base: float32 [400, 256], P('region'), may hold values from 0.5 to 2
- demand_pattern: float32 [16, 256], replicated, may hold values from 0.5 to 2
- demand_index: int32 [4, 400, 2], P('scen', 'region', 'day'), may hold values from 0 to 15
- initial_stock: float32 [400, 5, 256], P('region'), may hold values from 0 to 2
- depot_supply: float32 [60, 2, 256], P('region', 'day'), may hold values from 4 to 16
- lane_cost: float32 [4, 4, 128], replicated, may hold values from 0.1 to 1
- item_volume: float32 [256], replicated, may hold values from 0.5 to 2
- holding_cost: float32 [6, 256], replicated, may hold values from 0.05 to 0.5
- unit_price: float32 [256], replicated, may hold values from 1 to 4
- short_penalty: float32 [256], replicated, may hold values from 2 to 8
- order_cost: float32 [256], replicated, may hold values from 0.5 to 2
- lane_depot: int32 [4, 4, 128], replicated, may hold values from 0 to 14
- lane_store: int32 [4, 4, 128], replicated, may hold values from 0 to 99
- lane_mask: int32 [4, 4, 128], replicated, may hold values 0 or 1
Outputs:
- shipments: float32 [4, 4, 4, 128, 2, 256], P('scen', 'region', None, None, 'day')
- holdings: float32 [4, 400, 2, 6, 256], P('scen', 'region', 'day')
- selling: float32 [4, 400, 2, 6, 256], P('scen', 'region', 'day')
- ordering: float32 [60, 256], P('region')
- balance_dual: float32 [4, 400, 2, 6, 256], P('scen', 'region', 'day')
- depot_dual: float32 [4, 60, 2, 256], P('scen', 'region', 'day')
The draws below stay inside these ranges and needn't reach their ends.
All inputs are finite; a program needn't handle non-finite values.
Results may differ from the reference program's by a relative error of at most 0.0003.
Values sent between devices are 32-bit elements; how exact they have to be, the bound alone decides.
A program may use at most 128 MiB of HBM per device.

```python
import math
import jax
import jax.numpy as jnp
from jax import lax

SKUS = 256
STORE_REG = 100
DC_REG = 15
LANES = 128
AGES = 6
PATTERNS = 16
ITERS = 4
DAYS = 2
REGIONS = 4
SCEN = 4
STORES = 400
DCS = 60


def touch_ends(entries, own_key, least, high):
    place = [jax.random.randint(jax.random.fold_in(own_key, axis), (), 0, length) for axis, length in enumerate(entries.shape)]
    longest = entries.shape.index(max(entries.shape))
    neighbour = place[:longest] + [(place[longest] + 1) % entries.shape[longest]] + place[longest + 1:]
    return entries.at[tuple(place)].set(least).at[tuple(neighbour)].set(high)


def block_levels(own_key, extent, split, low, largest):
    factor_of, own = 1.0, jax.random.fold_in(own_key, 6)
    for dim, blocks in split:
        draws = jnp.exp(jax.random.uniform(jax.random.fold_in(own, dim), (blocks,), jnp.float32, low / len(split), largest / len(split)))
        factor_of = factor_of * jnp.repeat(draws, extent[dim] // blocks).reshape([-1 if axis == dim else 1 for axis in range(len(extent))])
    return factor_of


def bell_draw(stream_key, shape, scale, limit, cuts=(), kind=jnp.bfloat16):
    result = scale * jax.random.normal(stream_key, shape, jnp.float32)
    if cuts:
        result = result * block_levels(stream_key, shape, cuts, -0.22, 0.18)
    return jnp.clip(result, -limit, limit).astype(kind)


def setup_inputs(seed: int = 0) -> dict:
    keys = jax.random.split(jax.random.key(seed), 23)
    return {
        "shipments_init": jnp.clip(1.0 * jax.random.uniform(keys[0], (SCEN, REGIONS, REGIONS, LANES, DAYS, SKUS), jnp.float32) ** block_levels(keys[0], (SCEN, REGIONS, REGIONS, LANES, DAYS, SKUS), ((0, 4), (1, 4), (4, 2)), -0.2, 0.2), 0.0, 1.0),
        "holdings_init": jnp.clip(2.0 * jax.random.uniform(keys[1], (SCEN, STORES, DAYS, AGES, SKUS), jnp.float32) ** block_levels(keys[1], (SCEN, STORES, DAYS, AGES, SKUS), ((0, 4), (1, 4), (2, 2)), -0.2, 0.2), 0.0, 2.0),
        "selling_init": jnp.clip(1.0 * jax.random.uniform(keys[2], (SCEN, STORES, DAYS, AGES, SKUS), jnp.float32) ** block_levels(keys[2], (SCEN, STORES, DAYS, AGES, SKUS), ((0, 4), (1, 4), (2, 2)), -0.2, 0.2), 0.0, 1.0),
        "shortage_init": jnp.clip(1.0 * jax.random.uniform(keys[3], (SCEN, STORES, DAYS, SKUS), jnp.float32) ** block_levels(keys[3], (SCEN, STORES, DAYS, SKUS), ((0, 4), (1, 4), (2, 2)), -0.2, 0.2), 0.0, 1.0),
        "ordering_init": jnp.clip(20.0 * jax.random.uniform(keys[4], (DCS, SKUS), jnp.float32) ** block_levels(keys[4], (DCS, SKUS), ((0, 4),), -0.2, 0.2), 0.0, 20.0),
        "balance_dual_init": bell_draw(keys[5], (SCEN, STORES, DAYS, AGES, SKUS), 0.5, 3.0, ((0, 4), (1, 4), (2, 2)), jnp.float32),
        "demand_dual_init": bell_draw(keys[6], (SCEN, STORES, DAYS, SKUS), 0.5, 3.0, ((0, 4), (1, 4), (2, 2)), jnp.float32),
        "depot_dual_init": jnp.clip(0.1 * jax.random.uniform(keys[7], (SCEN, DCS, DAYS, SKUS), jnp.float32) ** block_levels(keys[7], (SCEN, DCS, DAYS, SKUS), ((0, 4), (1, 4), (2, 2)), -0.2, 0.2), 0.0, 0.1),
        "demand_base": jnp.clip(jnp.exp(math.log(2.0) - 1.3862944 * jax.random.uniform(keys[8], (STORES, SKUS), jnp.float32) ** block_levels(keys[8], (STORES, SKUS), ((0, 4),), -0.2, 0.2)), 0.5, 2.0),
        "demand_pattern": jnp.clip(jnp.exp(jax.random.uniform(keys[9], (PATTERNS, SKUS), jnp.float32, math.log(0.5), math.log(2.0))), 0.5, 2.0),
        "demand_index": touch_ends(jax.random.randint(keys[10], (SCEN, STORES, DAYS), 0, PATTERNS), jax.random.fold_in(keys[10], 1), 0, PATTERNS - 1).astype(jnp.int32),
        "initial_stock": jnp.clip(2.0 * jax.random.uniform(keys[11], (STORES, AGES - 1, SKUS), jnp.float32) ** block_levels(keys[11], (STORES, AGES - 1, SKUS), ((0, 4),), -0.2, 0.2), 0.0, 2.0),
        "depot_supply": jnp.clip(jnp.exp(math.log(16.0) - 1.3862944 * jax.random.uniform(keys[12], (DCS, DAYS, SKUS), jnp.float32) ** block_levels(keys[12], (DCS, DAYS, SKUS), ((0, 4), (1, 2)), -0.2, 0.2)), 4.0, 16.0),
        "lane_cost": jnp.clip(jnp.exp(jax.random.uniform(keys[13], (REGIONS, REGIONS, LANES), jnp.float32, math.log(0.1), math.log(1.0))), 0.1, 1.0),
        "item_volume": jnp.clip(jnp.exp(jax.random.uniform(keys[14], (SKUS,), jnp.float32, math.log(0.5), math.log(2.0))), 0.5, 2.0),
        "holding_cost": jnp.clip(jnp.exp(jax.random.uniform(keys[15], (AGES, SKUS), jnp.float32, math.log(0.05), math.log(0.5))), 0.05, 0.5),
        "unit_price": jnp.clip(jnp.exp(jax.random.uniform(keys[16], (SKUS,), jnp.float32, math.log(1.0), math.log(4.0))), 1.0, 4.0),
        "short_penalty": jnp.clip(jnp.exp(jax.random.uniform(keys[17], (SKUS,), jnp.float32, math.log(2.0), math.log(8.0))), 2.0, 8.0),
        "order_cost": jnp.clip(jnp.exp(jax.random.uniform(keys[18], (SKUS,), jnp.float32, math.log(0.5), math.log(2.0))), 0.5, 2.0),
        "lane_depot": touch_ends(jax.random.randint(keys[19], (REGIONS, REGIONS, LANES), 0, DC_REG), jax.random.fold_in(keys[19], 1), 0, DC_REG - 1).astype(jnp.int32),
        "lane_store": touch_ends(jax.random.randint(keys[20], (REGIONS, REGIONS, LANES), 0, STORE_REG), jax.random.fold_in(keys[20], 1), 0, STORE_REG - 1).astype(jnp.int32),
        "lane_mask": touch_ends((jax.random.randint(keys[21], (REGIONS, REGIONS, LANES), 0, 5) < 3).astype(jnp.int32), jax.random.fold_in(keys[21], 1), 0, 1),
    }


primal_step = 0.25
order_step = 0.05
dual_step = 0.25
depot_step = 0.02


def reference(shipments_init, holdings_init, selling_init, shortage_init, ordering_init, balance_dual_init, demand_dual_init, depot_dual_init, demand_base, demand_pattern, demand_index, initial_stock, depot_supply, lane_cost, item_volume, holding_cost, unit_price, short_penalty, order_cost, lane_depot, lane_store, lane_mask):
    highest = lax.Precision.HIGHEST
    lane_weight = lane_mask.astype(jnp.float32)
    store_table = (lane_store[..., None] == jnp.arange(STORE_REG, dtype=jnp.int32)).astype(jnp.float32) * lane_weight[..., None]
    depot_table = (lane_depot[..., None] == jnp.arange(DC_REG, dtype=jnp.int32)).astype(jnp.float32) * lane_weight[..., None]
    pattern_table = (demand_index[..., None] == jnp.arange(PATTERNS, dtype=jnp.int32)).astype(jnp.float32)
    demand = jnp.einsum('nsdp,pk->nsdk', pattern_table, demand_pattern, precision=highest) * demand_base[None, :, None, :]
    lane_price = lane_cost[:, :, :, None, None] * item_volume
    keep_lanes = lane_weight[None, :, :, :, None, None]
    shipments, holdings, selling, shortage = shipments_init, holdings_init, selling_init, shortage_init
    ordering = ordering_init
    balance_dual, demand_dual, depot_dual = balance_dual_init, demand_dual_init, depot_dual_init
    for iterate in range(ITERS):
        first_age = balance_dual[:, :, :, 0, :].reshape(SCEN, REGIONS, STORE_REG, DAYS, SKUS)
        store_lanes = jnp.einsum('abls,nbstk->nabltk', store_table, first_age, precision=highest)
        depot_after = jnp.flip(jnp.cumsum(jnp.flip(depot_dual, 2), 2), 2).reshape(SCEN, REGIONS, DC_REG, DAYS, SKUS)
        depot_lanes = jnp.einsum('abld,nadtk->nabltk', depot_table, depot_after, precision=highest)
        next_dual = jnp.pad(balance_dual[:, :, 1:, 1:, :], ((0, 0), (0, 0), (0, 1), (0, 1), (0, 0)))
        new_ship = keep_lanes * jnp.maximum(0.0, shipments - primal_step * (lane_price + store_lanes + depot_lanes))
        new_hold = jnp.maximum(0.0, holdings - primal_step * (holding_cost - balance_dual + next_dual))
        new_sell = jnp.maximum(0.0, selling - primal_step * (-unit_price - balance_dual - demand_dual[:, :, :, None, :]))
        new_short = jnp.maximum(0.0, shortage - primal_step * (short_penalty - demand_dual))
        new_order = jnp.maximum(0.0, ordering - order_step * (order_cost - jnp.sum(depot_dual, axis=(0, 2))))
        ship_bar = 2.0 * new_ship - shipments
        hold_bar = 2.0 * new_hold - holdings
        sell_bar = 2.0 * new_sell - selling
        short_bar = 2.0 * new_short - shortage
        order_bar = 2.0 * new_order - ordering
        shipments, holdings, selling, shortage, ordering = new_ship, new_hold, new_sell, new_short, new_order
        arrivals = jnp.einsum('abls,nabltk->nbstk', store_table, ship_bar, precision=highest).reshape(SCEN, STORES, DAYS, SKUS)
        outflow = jnp.einsum('abld,nabltk->nadtk', depot_table, ship_bar, precision=highest).reshape(SCEN, DCS, DAYS, SKUS)
        starting = jnp.broadcast_to(initial_stock[None, :, None, :, :], (SCEN, STORES, 1, AGES - 1, SKUS))
        earlier = jnp.concatenate([starting, hold_bar[:, :, :-1, :-1, :]], axis=2)
        carried = jnp.concatenate([arrivals[:, :, :, None, :], earlier], axis=3)
        balance_dual = balance_dual - dual_step * (hold_bar + sell_bar - carried)
        demand_dual = demand_dual + dual_step * (demand - jnp.sum(sell_bar, axis=3) - short_bar)
        net_flow = outflow - depot_supply[None]
        depot_dual = jnp.maximum(0.0, depot_dual + depot_step * (jnp.cumsum(net_flow, axis=2) - order_bar[None, :, None, :]))
    return shipments, holdings, selling, ordering, balance_dual, depot_dual
```

```python
import functools

import jax
import jax.numpy as jnp
from jax import lax
from jax.experimental import pallas as pl
from jax.experimental.pallas import tpu as pltpu
from jax.sharding import PartitionSpec as P

ITERS = 4

primal_step = 0.25
order_step = 0.05
dual_step = 0.25
depot_step = 0.02


def round_up(value, step):
    return (value + step - 1) // step * step


def split_bf16(value):
    high = value.astype(jnp.bfloat16)
    low = (value - high.astype(jnp.float32)).astype(jnp.bfloat16)
    return high, low


def dot(a, b):
    return jnp.dot(a, b, preferred_element_type=jnp.float32)


def kernel(
    sizes,
    ship_in,
    hold_in,
    sell_in,
    short_in,
    order_in,
    bal_in,
    dem_in,
    dep_in,
    base_in,
    pattern_in,
    index_in,
    stock_in,
    supply_in,
    cost_ref,
    volume_ref,
    hcost_ref,
    price_ref,
    penalty_ref,
    ocost_ref,
    ldepot_ref,
    lstore_ref,
    lmask_ref,
    ship_out,
    hold_out,
    sell_out,
    order_out,
    bal_out,
    dep_out,
    ship,
    hold,
    sell,
    bal,
    held_bar,
    short,
    dem,
    demand,
    base,
    pattern,
    index,
    stock,
    supply,
    order,
    dep,
    lane_price,
    keep,
    into_lanes,
    from_lanes,
    prices,
    bar_high,
    bar_low,
    flow_send,
    flow_recv,
    after,
    block,
    local_sem,
    part_send,
    part_recv,
    tile_send,
    tile_recv,
    flow_ssem,
    flow_rsem,
    after_ssem,
    after_rsem,
    block_ssem,
    block_rsem,
    out_local,
    out_psend,
    out_precv,
    out_tsend,
    out_trecv,
):
    D, R, S, stores, depots, lanes, ages, K = sizes
    SP = round_up(stores, 128)
    DP = round_up(depots, 8)
    day, region, scen = lax.axis_index("day"), lax.axis_index("region"), lax.axis_index("scen")

    def turn(position, offset, count):
        return lax.rem(position + offset + count, count)

    def part(which):
        return pl.ds(pl.multiple_of(which * K, K), K)

    def to_peer(src, dst, ssem, rsem, where):
        return pltpu.make_async_remote_copy(
            src_ref=src,
            dst_ref=dst,
            send_sem=ssem,
            recv_sem=rsem,
            device_id=where,
            device_id_type=pl.DeviceIdType.MESH,
        )

    moves = [
        (lambda k: dep_in.at[:, 0, k], lambda t: dep.at[t]),
        (lambda k: supply_in.at[:, 0, k], lambda t: supply.at[t]),
    ]
    for a in range(ages):
        moves.append((lambda k, a=a: bal_in.at[:, a, 0, k], lambda t, a=a: bal.at[t, a]))
    moves.append((lambda k: dem_in.at[:, 0, k], lambda t: dem.at[t]))
    for a in range(ages):
        moves.append((lambda k, a=a: hold_in.at[:, a, 0, k], lambda t, a=a: hold.at[t, a]))
    for a in range(ages):
        moves.append((lambda k, a=a: sell_in.at[:, a, 0, k], lambda t, a=a: sell.at[t, a]))
    moves.append((lambda k: short_in.at[:, 0, k], lambda t: short.at[t]))
    moves.append((lambda k: index_in, lambda t: index.at[t]))

    mine = part(day)
    started = []
    for i, (src, dst) in enumerate(moves):
        started.append(pltpu.make_async_copy(src(mine), dst(day), local_sem.at[i]))
    extra = [
        (order_in.at[:, mine], order),
        (base_in.at[:, mine], base),
        (pattern_in.at[:, mine], pattern),
        (stock_in.at[:, :, mine], stock),
    ]
    for i, (src, dst) in enumerate(extra):
        started.append(pltpu.make_async_copy(src, dst, local_sem.at[len(moves) + i]))

    def tile(a):
        return pl.ds(pl.multiple_of(a * lanes, lanes), lanes)

    started.append(
        pltpu.make_async_copy(
            ship_in.at[tile(region), 0, mine],
            ship.at[tile(region), part(day)],
            local_sem.at[len(moves) + len(extra)],
        )
    )
    for copy in started:
        copy.start()

    barrier = pltpu.get_barrier_semaphore()
    count = 0
    for dc in range(D):
        for dr in range(R):
            if dc or dr:
                pl.semaphore_signal(
                    barrier,
                    inc=1,
                    device_id=(turn(day, dc, D), turn(region, dr, R), scen),
                    device_id_type=pl.DeviceIdType.MESH,
                )
                count += 1
    for ds in range(1, S):
        pl.semaphore_signal(
            barrier,
            inc=1,
            device_id=(day, region, turn(scen, ds, S)),
            device_id_type=pl.DeviceIdType.MESH,
        )
        count += 1
    pl.semaphore_wait(barrier, count)

    sends = []
    recvs = []

    def exchange(src_of, dst_of, ssem, rsem, dc, dr):
        to = (turn(day, dc, D), turn(region, dr, R), scen)
        out = to_peer(src_of(to[0], to[1]), dst_of(day, region), ssem, rsem, to)
        out.start()
        sends.append(out)
        back = (turn(day, -dc, D), turn(region, -dr, R), scen)
        return to_peer(src_of(to[0], to[1]), dst_of(back[0], back[1]), ssem, rsem, back)

    def ship_tiles(dc, dr):
        return exchange(
            lambda t, a: ship_in.at[tile(a), 0, part(t)],
            lambda t, a: ship.at[tile(a), part(t)],
            tile_send.at[dc, dr],
            tile_recv.at[dc, dr],
            dc,
            dr,
        )

    ship_recv = []
    for dr in range(1, R):
        for dc in range(D):
            ship_recv.append(ship_tiles(dc, dr))
    part_recvs = []
    for i, (src, dst) in enumerate(moves):
        for dc in range(1, D):
            part_recvs.append(
                exchange(
                    lambda t, a, src=src: src(part(t)),
                    lambda t, a, dst=dst: dst(t),
                    part_send.at[i, dc],
                    part_recv.at[i, dc],
                    dc,
                    0,
                )
            )
    for dc in range(1, D):
        ship_recv.append(ship_tiles(dc, 0))

    lane_ids = lax.broadcasted_iota(jnp.int32, (lanes, SP), 1).astype(jnp.float32)
    side_ids = lax.broadcasted_iota(jnp.int32, (lanes, R * DP), 1).astype(jnp.float32)
    store_ids = lax.broadcasted_iota(jnp.int32, (SP, lanes), 0).astype(jnp.float32)
    depot_ids = lax.broadcasted_iota(jnp.int32, (R * DP, lanes), 0).astype(jnp.float32)
    volume = volume_ref[:, mine]
    own = pl.ds(region, 1)
    for a in range(R):
        rows = slice(a * lanes, (a + 1) * lanes)
        store_row = lstore_ref[a, own, :].astype(jnp.float32)
        depot_row = ldepot_ref[a, own, :].astype(jnp.float32) + float(a * DP)
        weight_row = lmask_ref[a, own, :].astype(jnp.float32)
        cost_row = cost_ref[a, own, :]

        def column(row):
            return jnp.broadcast_to(row, (lanes, lanes)).T

        weight = column(weight_row)
        keep[rows, :] = weight[:, :K]
        lane_price[rows, :] = column(cost_row)[:, :1] * volume
        weight = weight[:, :1]
        into_lanes[rows, 0:SP] = jnp.where(
            lane_ids == column(store_row)[:, :1], weight, 0.0
        ).astype(jnp.bfloat16)
        into_lanes[rows, SP : SP + R * DP] = jnp.where(
            side_ids == column(depot_row)[:, :1], weight, 0.0
        ).astype(jnp.bfloat16)
        from_lanes[0:SP, rows] = jnp.where(store_ids == store_row, weight_row, 0.0).astype(
            jnp.bfloat16
        )
        from_lanes[SP : SP + R * DP, rows] = jnp.where(
            depot_ids == depot_row, weight_row, 0.0
        ).astype(jnp.bfloat16)
    prices[...] = jnp.zeros_like(prices)

    for copy in started:
        copy.wait()
    for copy in part_recvs[: 2 * (D - 1)]:
        copy.wait_recv()

    def send_after(it):
        total = dep[0]
        for t in range(1, D):
            total = total + dep[t]
        block[it, scen] = total
        later = dep[D - 1]
        after[it, region, D - 1] = later
        for t in reversed(range(D - 1)):
            later = later + dep[t]
            after[it, region, t] = later
        waits = []
        for dr in range(1, R):
            waits.append(
                exchange(
                    lambda t, a: after.at[it, region],
                    lambda t, a: after.at[it, a],
                    after_ssem.at[it, dr],
                    after_rsem.at[it, dr],
                    0,
                    dr,
                )
            )
        totals = []
        for ds in range(1, S):
            out = to_peer(
                block.at[it, scen],
                block.at[it, scen],
                block_ssem.at[it, ds],
                block_rsem.at[it, ds],
                (day, region, turn(scen, ds, S)),
            )
            out.start()
            sends.append(out)
            back = turn(scen, -ds, S)
            totals.append(
                to_peer(
                    block.at[it, back],
                    block.at[it, back],
                    block_ssem.at[it, ds],
                    block_rsem.at[it, ds],
                    (day, region, back),
                )
            )
        return waits, totals

    after_recv, block_recv = send_after(0)

    for copy in part_recvs[2 * (D - 1) :]:
        copy.wait_recv()

    pattern_ids = lax.broadcasted_iota(jnp.int32, (pattern.shape[0], stores), 0)
    table = pattern[...]
    for t in range(D):
        chosen = (pattern_ids == index[t]).astype(jnp.float32)
        demand[t] = (
            lax.dot_general(
                chosen,
                table,
                (((0,), (0,)), ((), ())),
                precision=lax.Precision.HIGHEST,
                preferred_element_type=jnp.float32,
            )
            * base[...]
        )

    hcost = hcost_ref[:, mine]
    unit_price = price_ref[:, mine]
    penalty = penalty_ref[:, mine]
    order_cost = ocost_ref[:, mine]

    def step_stores(t):
        price = dem[t]
        sold = jnp.zeros_like(price)
        for a in reversed(range(ages)):
            b, h, s = bal[t, a], hold[t, a], sell[t, a]
            slope = hcost[a : a + 1] - b
            if t + 1 < D and a + 1 < ages:
                slope = slope + bal[t + 1, a + 1]
            new_hold = jnp.maximum(0.0, h - primal_step * slope)
            new_sell = jnp.maximum(0.0, s - primal_step * (-unit_price - b - price))
            hold_bar = 2.0 * new_hold - h
            sell_bar = 2.0 * new_sell - s
            sold = sold + sell_bar
            change = hold_bar + sell_bar
            if a >= 1:
                change = change - (stock[a - 1] if t == 0 else held_bar[a - 1])
            bal[t, a] = b - dual_step * change
            hold[t, a] = new_hold
            sell[t, a] = new_sell
            held_bar[a] = hold_bar
        lost = short[t]
        new_short = jnp.maximum(0.0, lost - primal_step * (penalty - price))
        short[t] = new_short
        dem[t] = price + dual_step * (demand[t] - sold - (2.0 * new_short - lost))

    out_sends = []
    out_waits = []

    def put(i, array, out, t_ref):
        local = pltpu.make_async_copy(t_ref(day), out(mine), out_local.at[i])
        local.start()
        out_waits.append(local)
        for dc in range(1, D):
            to = (turn(day, dc, D), region, scen)
            go = to_peer(
                t_ref(to[0]), out(mine), out_psend.at[i, dc], out_precv.at[i, dc], to
            )
            go.start()
            out_sends.append(go)
            back = turn(day, -dc, D)
            recvs.append(
                to_peer(
                    t_ref(to[0]),
                    out(part(back)),
                    out_psend.at[i, dc],
                    out_precv.at[i, dc],
                    (back, region, scen),
                )
            )

    def put_ages(base_slot, array, out, which):
        for a in which:
            put(
                base_slot + a,
                array,
                lambda k, a=a: out.at[:, a, 0, k],
                lambda t, a=a: array.at[t, a],
            )

    for it in range(ITERS):
        final = it == ITERS - 1
        for t in range(D):
            prices[0:stores, t * K : (t + 1) * K] = bal[t, 0]
        early = D if it == 0 or final else 1
        for t in range(early):
            step_stores(t)
        if final:
            put_ages(0, hold, hold_out, range(ages))
            put_ages(ages, sell, sell_out, range(ages))
            put_ages(2 * ages, bal, bal_out, range(1, ages))
        if it == 0:
            for copy in ship_recv:
                copy.wait_recv()
        for copy in after_recv:
            copy.wait_recv()
        for a in range(R):
            for t in range(D):
                prices[SP + a * DP : SP + a * DP + depots, t * K : (t + 1) * K] = after[it, a, t]
        high, low = split_bf16(prices[...])
        for a in range(R):
            rows = slice(a * lanes, (a + 1) * lanes)
            spread = into_lanes[rows, :]
            cost = dot(spread, high) + dot(spread, low)
            for t in range(D):
                cols = slice(t * K, (t + 1) * K)
                old = ship[rows, cols]
                new = keep[rows, :] * jnp.maximum(
                    0.0, old - primal_step * (lane_price[rows, :] + cost[:, cols])
                )
                ship[rows, cols] = new
                bar = split_bf16(2.0 * new - old)
                bar_high[rows, cols] = bar[0]
                bar_low[rows, cols] = bar[1]
        gather = from_lanes[SP:, :]
        flow = dot(gather, bar_high[...]) + dot(gather, bar_low[...])
        for a in range(R):
            flow_send[it, a] = flow[a * DP : (a + 1) * DP, :]
        flow_waits = []
        for dr in range(1, R):
            flow_waits.append(
                exchange(
                    lambda t, a: flow_send.at[it, a],
                    lambda t, a: flow_recv.at[it, dr],
                    flow_ssem.at[it, dr],
                    flow_rsem.at[it, dr],
                    0,
                    dr,
                )
            )
        if final:
            for dr in list(range(1, R)) + [0]:
                for dc in range(D):
                    if dc == 0 and dr == 0:
                        local = pltpu.make_async_copy(
                            ship.at[tile(region), part(day)],
                            ship_out.at[tile(region), 0, mine],
                            out_local.at[3 * ages],
                        )
                        local.start()
                        out_waits.append(local)
                        continue
                    recvs.append(
                        exchange(
                            lambda t, a: ship.at[tile(a), part(t)],
                            lambda t, a: ship_out.at[tile(a), 0, part(t)],
                            out_tsend.at[dc, dr],
                            out_trecv.at[dc, dr],
                            dc,
                            dr,
                        )
                    )
        for t in range(early, D):
            step_stores(t)
        gather = from_lanes[0:SP, :]
        arrivals = dot(gather, bar_high[...]) + dot(gather, bar_low[...])
        for t in range(D):
            bal[t, 0] = bal[t, 0] + dual_step * arrivals[0:stores, t * K : (t + 1) * K]
        if final:
            put_ages(2 * ages, bal, bal_out, range(1))
        for copy in block_recv:
            copy.wait_recv()
        total = block[it, 0]
        for n in range(1, S):
            total = total + block[it, n]
        old = order[...]
        new = jnp.maximum(0.0, old - order_step * (order_cost - total))
        order[...] = new
        order_bar = 2.0 * new - old
        if final:
            put(3 * ages + 1, order, lambda k: order_out.at[:, k], lambda t: order)
        for copy in flow_waits:
            copy.wait_recv()
        outflow = flow_send[it, region]
        for dr in range(1, R):
            outflow = outflow + flow_recv[it, dr]
        running = -order_bar
        for t in range(D):
            running = running + (outflow[0:depots, t * K : (t + 1) * K] - supply[t])
            dep[t] = jnp.maximum(0.0, dep[t] + depot_step * running)
        if final:
            put(3 * ages + 2, dep, lambda k: dep_out.at[:, 0, k], lambda t: dep.at[t])
        else:
            after_recv, block_recv = send_after(it + 1)

    for copy in recvs:
        copy.wait_recv()
    for copy in sends + out_sends:
        copy.wait_send()
    for copy in out_waits:
        copy.wait()


def per_device(
    D,
    R,
    S,
    shipments_init,
    holdings_init,
    selling_init,
    shortage_init,
    ordering_init,
    balance_dual_init,
    demand_dual_init,
    depot_dual_init,
    demand_base,
    demand_pattern,
    demand_index,
    initial_stock,
    depot_supply,
    lane_cost,
    item_volume,
    holding_cost,
    unit_price,
    short_penalty,
    order_cost,
    lane_depot,
    lane_store,
    lane_mask,
):
    _, stores, local_days, ages, items = holdings_init.shape
    assert local_days == 1 and items % D == 0
    depots = depot_dual_init.shape[1]
    lanes = shipments_init.shape[3]
    K = items // D
    f32 = jnp.float32
    SP = round_up(stores, 128)
    DP = round_up(depots, 8)
    any_ = pl.BlockSpec(memory_space=pl.ANY)
    vmem = pl.BlockSpec(memory_space=pltpu.VMEM)
    moved = 4 + 3 * ages + 1
    DMA = pltpu.SemaphoreType.DMA
    rows = R * lanes
    outs = pl.pallas_call(
        functools.partial(kernel, (D, R, S, stores, depots, lanes, ages, K)),
        out_shape=(
            jax.ShapeDtypeStruct((rows, 1, items), f32),
            jax.ShapeDtypeStruct((stores, ages, 1, items), f32),
            jax.ShapeDtypeStruct((stores, ages, 1, items), f32),
            jax.ShapeDtypeStruct((depots, items), f32),
            jax.ShapeDtypeStruct((stores, ages, 1, items), f32),
            jax.ShapeDtypeStruct((depots, 1, items), f32),
        ),
        in_specs=[any_] * 13 + [vmem] * 9,
        out_specs=(any_,) * 6,
        scratch_shapes=[
            pltpu.VMEM((rows, D * K), f32),
            pltpu.VMEM((D, ages, stores, K), f32),
            pltpu.VMEM((D, ages, stores, K), f32),
            pltpu.VMEM((D, ages, stores, K), f32),
            pltpu.VMEM((ages, stores, K), f32),
            pltpu.VMEM((D, stores, K), f32),
            pltpu.VMEM((D, stores, K), f32),
            pltpu.VMEM((D, stores, K), f32),
            pltpu.VMEM((stores, K), f32),
            pltpu.VMEM((demand_pattern.shape[0], K), f32),
            pltpu.VMEM((D, 1, stores), jnp.int32),
            pltpu.VMEM((ages - 1, stores, K), f32),
            pltpu.VMEM((D, depots, K), f32),
            pltpu.VMEM((depots, K), f32),
            pltpu.VMEM((D, depots, K), f32),
            pltpu.VMEM((rows, K), f32),
            pltpu.VMEM((rows, K), f32),
            pltpu.VMEM((rows, SP + R * DP), jnp.bfloat16),
            pltpu.VMEM((SP + R * DP, rows), jnp.bfloat16),
            pltpu.VMEM((SP + R * DP, D * K), f32),
            pltpu.VMEM((rows, D * K), jnp.bfloat16),
            pltpu.VMEM((rows, D * K), jnp.bfloat16),
            pltpu.VMEM((ITERS, R, DP, D * K), f32),
            pltpu.VMEM((ITERS, R, DP, D * K), f32),
            pltpu.VMEM((ITERS, R, D, depots, K), f32),
            pltpu.VMEM((ITERS, S, depots, K), f32),
            DMA((moved + 5,)),
            DMA((moved, D)),
            DMA((moved, D)),
            DMA((D, R)),
            DMA((D, R)),
            DMA((ITERS, R)),
            DMA((ITERS, R)),
            DMA((ITERS, R)),
            DMA((ITERS, R)),
            DMA((ITERS, S)),
            DMA((ITERS, S)),
            DMA((3 * ages + 3,)),
            DMA((3 * ages + 3, D)),
            DMA((3 * ages + 3, D)),
            DMA((D, R)),
            DMA((D, R)),
        ],
        compiler_params=pltpu.CompilerParams(collective_id=0, has_side_effects=True),
    )(
        shipments_init.reshape(rows, 1, items),
        holdings_init.reshape(stores, ages, 1, items),
        selling_init.reshape(stores, ages, 1, items),
        shortage_init.reshape(stores, 1, items),
        ordering_init,
        balance_dual_init.reshape(stores, ages, 1, items),
        demand_dual_init.reshape(stores, 1, items),
        depot_dual_init.reshape(depots, 1, items),
        demand_base,
        demand_pattern,
        demand_index.reshape(1, stores),
        jnp.transpose(initial_stock, (1, 0, 2)),
        depot_supply.reshape(depots, 1, items),
        lane_cost,
        item_volume.reshape(1, items),
        holding_cost,
        unit_price.reshape(1, items),
        short_penalty.reshape(1, items),
        order_cost.reshape(1, items),
        lane_depot,
        lane_store,
        lane_mask,
    )
    return (
        outs[0].reshape(shipments_init.shape),
        outs[1].reshape(holdings_init.shape),
        outs[2].reshape(holdings_init.shape),
        outs[3],
        outs[4].reshape(holdings_init.shape),
        outs[5].reshape(depot_dual_init.shape),
    )


def solution(mesh):
    placed = (
        P("scen", "region", None, None, "day", None),
        P("scen", "region", "day", None, None),
        P("scen", "region", "day", None, None),
        P("scen", "region", "day", None),
        P("region", None),
        P("scen", "region", "day", None, None),
        P("scen", "region", "day", None),
        P("scen", "region", "day", None),
        P("region", None),
        P(),
        P("scen", "region", "day"),
        P("region", None, None),
        P("region", "day", None),
        P(),
        P(),
        P(),
        P(),
        P(),
        P(),
        P(),
        P(),
        P(),
    )
    return jax.shard_map(
        functools.partial(
            per_device, mesh.shape["day"], mesh.shape["region"], mesh.shape["scen"]
        ),
        mesh=mesh,
        in_specs=placed,
        out_specs=(
            P("scen", "region", None, None, "day", None),
            P("scen", "region", "day", None, None),
            P("scen", "region", "day", None, None),
            P("region", None),
            P("scen", "region", "day", None, None),
            P("scen", "region", "day", None),
        ),
        check_vma=False,
    )
```

```python
import functools

import jax
import jax.numpy as jnp
from jax import lax
from jax.experimental import pallas as pl
from jax.experimental.pallas import tpu as pltpu
from jax.sharding import PartitionSpec as P

ITERS = 4

primal_step = 0.25
order_step = 0.05
dual_step = 0.25
depot_step = 0.02


def round_up(value, step):
    return (value + step - 1) // step * step


def split_bf16(value):
    high = value.astype(jnp.bfloat16)
    low = (value - high.astype(jnp.float32)).astype(jnp.bfloat16)
    return high, low


def dot(a, b):
    return jnp.dot(a, b, preferred_element_type=jnp.float32)


def kernel(
    sizes,
    ship_in,
    hold_in,
    sell_in,
    short_in,
    order_in,
    bal_in,
    dem_in,
    dep_in,
    base_in,
    pattern_in,
    index_in,
    stock_in,
    supply_in,
    cost_ref,
    volume_ref,
    hcost_ref,
    price_ref,
    penalty_ref,
    ocost_ref,
    ldepot_ref,
    lstore_ref,
    lmask_ref,
    ship_out,
    hold_out,
    sell_out,
    order_out,
    bal_out,
    dep_out,
    ship,
    hold,
    sell,
    bal,
    held_bar,
    short,
    dem,
    demand,
    base,
    pattern,
    index,
    stock,
    supply,
    order,
    dep,
    lane_price,
    keep,
    into_lanes,
    from_lanes,
    into_sides,
    from_sides,
    toll,
    prices,
    bar_high,
    bar_low,
    flow_send,
    flow_recv,
    after,
    block,
    local_sem,
    part_send,
    part_recv,
    tile_send,
    tile_recv,
    flow_ssem,
    flow_rsem,
    after_ssem,
    after_rsem,
    block_ssem,
    block_rsem,
    out_local,
    out_psend,
    out_precv,
    out_tsend,
    out_trecv,
):
    D, R, S, stores, depots, lanes, ages, K = sizes
    assert R & (R - 1) == 0
    SP = round_up(stores, 128)
    DP = round_up(depots, 16)
    day, region, scen = lax.axis_index("day"), lax.axis_index("region"), lax.axis_index("scen")

    def turn(position, offset, count):
        return lax.rem(position + offset + count, count)

    def partner(x):
        peer = region
        for bit in range(R.bit_length() - 1):
            if x >> bit & 1:
                peer = peer + (1 << bit) * (1 - 2 * ((region // (1 << bit)) % 2))
        return peer, peer

    def part(which):
        return pl.ds(pl.multiple_of(which * K, K), K)

    def to_peer(src, dst, ssem, rsem, where):
        return pltpu.make_async_remote_copy(
            src_ref=src,
            dst_ref=dst,
            send_sem=ssem,
            recv_sem=rsem,
            device_id=where,
            device_id_type=pl.DeviceIdType.MESH,
        )

    moves = [
        (lambda k: dep_in.at[:, 0, k], lambda t: dep.at[t]),
        (lambda k: supply_in.at[:, 0, k], lambda t: supply.at[t]),
        (lambda k: bal_in.at[:, 0, 0, k], lambda t: bal.at[t, 0]),
        (lambda k: dem_in.at[:, 0, k], lambda t: dem.at[t]),
        (lambda k: short_in.at[:, 0, k], lambda t: short.at[t]),
        (lambda k: index_in, lambda t: index.at[t]),
    ]
    for a in range(ages):
        if a:
            moves.append((lambda k, a=a: bal_in.at[:, a, 0, k], lambda t, a=a: bal.at[t, a]))
        moves.append((lambda k, a=a: hold_in.at[:, a, 0, k], lambda t, a=a: hold.at[t, a]))
        moves.append((lambda k, a=a: sell_in.at[:, a, 0, k], lambda t, a=a: sell.at[t, a]))
    first = 3

    mine = part(day)
    started = []
    for i, (src, dst) in enumerate(moves):
        started.append(pltpu.make_async_copy(src(mine), dst(day), local_sem.at[i]))
    extra = [
        (order_in.at[:, mine], order),
        (base_in.at[:, mine], base),
        (pattern_in.at[:, mine], pattern),
        (stock_in.at[:, :, mine], stock),
    ]
    for i, (src, dst) in enumerate(extra):
        started.append(pltpu.make_async_copy(src, dst, local_sem.at[len(moves) + i]))

    def tile(a):
        return pl.ds(pl.multiple_of(a * lanes, lanes), lanes)

    started.append(
        pltpu.make_async_copy(
            ship_in.at[tile(region), 0, mine],
            ship.at[tile(region), part(day)],
            local_sem.at[len(moves) + len(extra)],
        )
    )
    for copy in started:
        copy.start()

    barrier = pltpu.get_barrier_semaphore()
    count = 0
    for dc in range(D):
        for dr in range(R):
            if dc or dr:
                pl.semaphore_signal(
                    barrier,
                    inc=1,
                    device_id=(turn(day, dc, D), turn(region, dr, R), scen),
                    device_id_type=pl.DeviceIdType.MESH,
                )
                count += 1
    for ds in range(1, S):
        pl.semaphore_signal(
            barrier,
            inc=1,
            device_id=(day, region, turn(scen, ds, S)),
            device_id_type=pl.DeviceIdType.MESH,
        )
        count += 1
    pl.semaphore_wait(barrier, count)

    sends = []
    recvs = []

    def exchange(src_of, dst_of, ssem, rsem, dc, dr):
        ahead, behind = partner(dr)
        to = (turn(day, dc, D), ahead, scen)
        out = to_peer(src_of(to[0], to[1]), dst_of(day, region), ssem, rsem, to)
        out.start()
        sends.append(out)
        back = (turn(day, -dc, D), behind, scen)
        return to_peer(src_of(to[0], to[1]), dst_of(back[0], back[1]), ssem, rsem, back)

    def ship_tiles(dc, dr):
        return exchange(
            lambda t, a: ship_in.at[tile(a), 0, part(t)],
            lambda t, a: ship.at[tile(a), part(t)],
            tile_send.at[dc, dr],
            tile_recv.at[dc, dr],
            dc,
            dr,
        )

    part_recvs = []

    def move(which):
        for i in which:
            src, dst = moves[i]
            for dc in range(1, D):
                part_recvs.append(
                    exchange(
                        lambda t, a: src(part(t)),
                        lambda t, a: dst(t),
                        part_send.at[i, dc],
                        part_recv.at[i, dc],
                        dc,
                        0,
                    )
                )

    move(range(first))
    ship_recv = [[ship_tiles(dc, 0) for dc in range(1, D)]]
    for dr in range(1, R):
        ship_recv.append([ship_tiles(dc, dr) for dc in range(D)])
    move(range(first, len(moves)))

    lane_ids = lax.broadcasted_iota(jnp.int32, (lanes, SP), 1).astype(jnp.float32)
    side_ids = lax.broadcasted_iota(jnp.int32, (lanes, DP), 1).astype(jnp.float32)
    store_ids = lax.broadcasted_iota(jnp.int32, (SP, lanes), 0).astype(jnp.float32)
    depot_ids = lax.broadcasted_iota(jnp.int32, (DP, lanes), 0).astype(jnp.float32)
    volume = volume_ref[:, mine]
    own = pl.ds(region, 1)
    prices[...] = jnp.zeros_like(prices)
    for it in range(ITERS):
        after[it, region] = jnp.zeros((DP, D * K), jnp.float32)

    def local_wait(which):
        for i in which:
            started[i].wait()

    local_wait(range(first))
    for copy in part_recvs[: 2 * (D - 1)]:
        copy.wait_recv()

    def send_after(it):
        total = dep[0]
        for t in range(1, D):
            total = total + dep[t]
        block[it, scen] = total
        later = dep[D - 1]
        after[it, region, 0:depots, (D - 1) * K : D * K] = later
        for t in reversed(range(D - 1)):
            later = later + dep[t]
            after[it, region, 0:depots, t * K : (t + 1) * K] = later
        waits = []
        for dr in range(1, R):
            waits.append(
                exchange(
                    lambda t, a: after.at[it, region],
                    lambda t, a: after.at[it, a],
                    after_ssem.at[it, dr],
                    after_rsem.at[it, dr],
                    0,
                    dr,
                )
            )
        totals = []
        for ds in range(1, S):
            out = to_peer(
                block.at[it, scen],
                block.at[it, scen],
                block_ssem.at[it, ds],
                block_rsem.at[it, ds],
                (day, region, turn(scen, ds, S)),
            )
            out.start()
            sends.append(out)
            back = turn(scen, -ds, S)
            totals.append(
                to_peer(
                    block.at[it, back],
                    block.at[it, back],
                    block_ssem.at[it, ds],
                    block_rsem.at[it, ds],
                    (day, region, back),
                )
            )
        return waits, totals

    after_recv, block_recv = send_after(0)

    for a in range(R):
        rows = slice(a * lanes, (a + 1) * lanes)
        store_row = lstore_ref[a, own, :].astype(jnp.float32)
        depot_row = ldepot_ref[a, own, :].astype(jnp.float32)
        weight_row = lmask_ref[a, own, :].astype(jnp.float32)
        cost_row = cost_ref[a, own, :]

        def column(row):
            return jnp.broadcast_to(row, (lanes, lanes)).T

        weight = column(weight_row)
        keep[rows, :] = weight[:, :K]
        lane_price[rows, :] = column(cost_row)[:, :1] * volume
        weight = weight[:, :1]
        into_lanes[rows, :] = jnp.where(
            lane_ids == column(store_row)[:, :1], weight, 0.0
        ).astype(jnp.bfloat16)
        into_sides[a] = jnp.where(side_ids == column(depot_row)[:, :1], weight, 0.0).astype(
            jnp.bfloat16
        )
        from_lanes[:, rows] = jnp.where(store_ids == store_row, weight_row, 0.0).astype(
            jnp.bfloat16
        )
        from_sides[a] = jnp.where(depot_ids == depot_row, weight_row, 0.0).astype(jnp.bfloat16)

    for copy in part_recvs[2 * (D - 1) : first * (D - 1)]:
        copy.wait_recv()

    def set_demand():
        pattern_ids = lax.broadcasted_iota(jnp.int32, (pattern.shape[0], stores), 0)
        table = pattern[...]
        for t in range(D):
            chosen = (pattern_ids == index[t]).astype(jnp.float32)
            demand[t] = (
                lax.dot_general(
                    chosen,
                    table,
                    (((0,), (0,)), ((), ())),
                    precision=lax.Precision.HIGHEST,
                    preferred_element_type=jnp.float32,
                )
                * base[...]
            )

    hcost = hcost_ref[:, mine]
    unit_price = price_ref[:, mine]
    penalty = penalty_ref[:, mine]
    order_cost = ocost_ref[:, mine]

    def step_stores(t):
        price = dem[t]
        sold = jnp.zeros_like(price)
        for a in reversed(range(ages)):
            b, h, s = bal[t, a], hold[t, a], sell[t, a]
            slope = hcost[a : a + 1] - b
            if t + 1 < D and a + 1 < ages:
                slope = slope + bal[t + 1, a + 1]
            new_hold = jnp.maximum(0.0, h - primal_step * slope)
            new_sell = jnp.maximum(0.0, s - primal_step * (-unit_price - b - price))
            hold_bar = 2.0 * new_hold - h
            sell_bar = 2.0 * new_sell - s
            sold = sold + sell_bar
            change = hold_bar + sell_bar
            if a >= 1:
                change = change - (stock[a - 1] if t == 0 else held_bar[a - 1])
            bal[t, a] = b - dual_step * change
            hold[t, a] = new_hold
            sell[t, a] = new_sell
            held_bar[a] = hold_bar
        lost = short[t]
        new_short = jnp.maximum(0.0, lost - primal_step * (penalty - price))
        short[t] = new_short
        dem[t] = price + dual_step * (demand[t] - sold - (2.0 * new_short - lost))

    out_sends = []
    out_waits = []

    def put(i, array, out, t_ref):
        local = pltpu.make_async_copy(t_ref(day), out(mine), out_local.at[i])
        local.start()
        out_waits.append(local)
        for dc in range(1, D):
            to = (turn(day, dc, D), region, scen)
            go = to_peer(
                t_ref(to[0]), out(mine), out_psend.at[i, dc], out_precv.at[i, dc], to
            )
            go.start()
            out_sends.append(go)
            back = turn(day, -dc, D)
            recvs.append(
                to_peer(
                    t_ref(to[0]),
                    out(part(back)),
                    out_psend.at[i, dc],
                    out_precv.at[i, dc],
                    (back, region, scen),
                )
            )

    def put_ages(base_slot, array, out, which):
        for a in which:
            put(
                base_slot + a,
                array,
                lambda k, a=a: out.at[:, a, 0, k],
                lambda t, a=a: array.at[t, a],
            )

    for it in range(ITERS):
        final = it == ITERS - 1
        for t in range(D):
            prices[0:stores, t * K : (t + 1) * K] = bal[t, 0]
        early = D if final else 0 if it == 0 else 1
        high, low = split_bf16(prices[...])
        for a in range(R):
            rows = slice(a * lanes, (a + 1) * lanes)
            spread = into_lanes[rows, :]
            cost = dot(spread, high) + dot(spread, low)
            for t in range(D):
                cols = slice(t * K, (t + 1) * K)
                toll[rows, cols] = lane_price[rows, :] + cost[:, cols]
        for t in range(early):
            step_stores(t)
        if final:
            put_ages(0, hold, hold_out, range(ages))
            put_ages(ages, sell, sell_out, range(ages))
            put_ages(2 * ages, bal, bal_out, range(1, ages))
        flow_waits = []
        for x in range(R):
            a = partner(x)[1]
            if it == 0:
                for copy in ship_recv[x]:
                    copy.wait_recv()
                if x == 0:
                    local_wait([len(moves) + len(extra)])
            if x:
                after_recv[x - 1].wait_recv()
            rows = tile(a)
            high, low = split_bf16(after[it, a])
            spread = into_sides[a]
            cost = dot(spread, high) + dot(spread, low)
            weight = keep[rows, :]
            bars = []
            for t in range(D):
                cols = slice(t * K, (t + 1) * K)
                old = ship[rows, cols]
                new = weight * jnp.maximum(
                    0.0, old - primal_step * (toll[rows, cols] + cost[:, cols])
                )
                ship[rows, cols] = new
                bars.append(2.0 * new - old)
            high, low = split_bf16(jnp.concatenate(bars, axis=1))
            bar_high[rows, :] = high
            bar_low[rows, :] = low
            gather = from_sides[a]
            flow_send[it, a] = dot(gather, high) + dot(gather, low)
            if x:
                flow_waits.append(
                    exchange(
                        lambda t, a: flow_send.at[it, a],
                        lambda t, a: flow_recv.at[it, x],
                        flow_ssem.at[it, x],
                        flow_rsem.at[it, x],
                        0,
                        x,
                    )
                )
        if final:
            for dr in list(range(R - 1, 0, -1)) + [0]:
                for dc in range(D):
                    if dc == 0 and dr == 0:
                        local = pltpu.make_async_copy(
                            ship.at[tile(region), part(day)],
                            ship_out.at[tile(region), 0, mine],
                            out_local.at[3 * ages],
                        )
                        local.start()
                        out_waits.append(local)
                        continue
                    recvs.append(
                        exchange(
                            lambda t, a: ship.at[tile(a), part(t)],
                            lambda t, a: ship_out.at[tile(a), 0, part(t)],
                            out_tsend.at[dc, dr],
                            out_trecv.at[dc, dr],
                            dc,
                            dr,
                        )
                    )
        if it == 0:
            local_wait(range(first, len(moves) + len(extra)))
            for copy in part_recvs[first * (D - 1) :]:
                copy.wait_recv()
            set_demand()
        for t in range(early, D):
            step_stores(t)
        gather = from_lanes[...]
        arrivals = dot(gather, bar_high[...]) + dot(gather, bar_low[...])
        for t in range(D):
            bal[t, 0] = bal[t, 0] + dual_step * arrivals[0:stores, t * K : (t + 1) * K]
        if final:
            put_ages(2 * ages, bal, bal_out, range(1))
        for copy in block_recv:
            copy.wait_recv()
        total = block[it, 0]
        for n in range(1, S):
            total = total + block[it, n]
        old = order[...]
        new = jnp.maximum(0.0, old - order_step * (order_cost - total))
        order[...] = new
        order_bar = 2.0 * new - old
        if final:
            put(3 * ages + 1, order, lambda k: order_out.at[:, k], lambda t: order)
        for copy in flow_waits:
            copy.wait_recv()
        outflow = flow_send[it, region]
        for dr in range(1, R):
            outflow = outflow + flow_recv[it, dr]
        running = -order_bar
        for t in range(D):
            running = running + (outflow[0:depots, t * K : (t + 1) * K] - supply[t])
            dep[t] = jnp.maximum(0.0, dep[t] + depot_step * running)
        if final:
            put(3 * ages + 2, dep, lambda k: dep_out.at[:, 0, k], lambda t: dep.at[t])
        else:
            after_recv, block_recv = send_after(it + 1)

    for copy in recvs:
        copy.wait_recv()
    for copy in sends + out_sends:
        copy.wait_send()
    for copy in out_waits:
        copy.wait()


def per_device(
    D,
    R,
    S,
    shipments_init,
    holdings_init,
    selling_init,
    shortage_init,
    ordering_init,
    balance_dual_init,
    demand_dual_init,
    depot_dual_init,
    demand_base,
    demand_pattern,
    demand_index,
    initial_stock,
    depot_supply,
    lane_cost,
    item_volume,
    holding_cost,
    unit_price,
    short_penalty,
    order_cost,
    lane_depot,
    lane_store,
    lane_mask,
):
    _, stores, local_days, ages, items = holdings_init.shape
    assert local_days == 1 and items % D == 0
    depots = depot_dual_init.shape[1]
    lanes = shipments_init.shape[3]
    K = items // D
    f32 = jnp.float32
    SP = round_up(stores, 128)
    DP = round_up(depots, 16)
    any_ = pl.BlockSpec(memory_space=pl.ANY)
    vmem = pl.BlockSpec(memory_space=pltpu.VMEM)
    moved = 4 + 3 * ages + 1
    DMA = pltpu.SemaphoreType.DMA
    rows = R * lanes
    outs = pl.pallas_call(
        functools.partial(kernel, (D, R, S, stores, depots, lanes, ages, K)),
        out_shape=(
            jax.ShapeDtypeStruct((rows, 1, items), f32),
            jax.ShapeDtypeStruct((stores, ages, 1, items), f32),
            jax.ShapeDtypeStruct((stores, ages, 1, items), f32),
            jax.ShapeDtypeStruct((depots, items), f32),
            jax.ShapeDtypeStruct((stores, ages, 1, items), f32),
            jax.ShapeDtypeStruct((depots, 1, items), f32),
        ),
        in_specs=[any_] * 13 + [vmem] * 9,
        out_specs=(any_,) * 6,
        scratch_shapes=[
            pltpu.VMEM((rows, D * K), f32),
            pltpu.VMEM((D, ages, stores, K), f32),
            pltpu.VMEM((D, ages, stores, K), f32),
            pltpu.VMEM((D, ages, stores, K), f32),
            pltpu.VMEM((ages, stores, K), f32),
            pltpu.VMEM((D, stores, K), f32),
            pltpu.VMEM((D, stores, K), f32),
            pltpu.VMEM((D, stores, K), f32),
            pltpu.VMEM((stores, K), f32),
            pltpu.VMEM((demand_pattern.shape[0], K), f32),
            pltpu.VMEM((D, 1, stores), jnp.int32),
            pltpu.VMEM((ages - 1, stores, K), f32),
            pltpu.VMEM((D, depots, K), f32),
            pltpu.VMEM((depots, K), f32),
            pltpu.VMEM((D, depots, K), f32),
            pltpu.VMEM((rows, K), f32),
            pltpu.VMEM((rows, K), f32),
            pltpu.VMEM((rows, SP), jnp.bfloat16),
            pltpu.VMEM((SP, rows), jnp.bfloat16),
            pltpu.VMEM((R, lanes, DP), jnp.bfloat16),
            pltpu.VMEM((R, DP, lanes), jnp.bfloat16),
            pltpu.VMEM((rows, D * K), f32),
            pltpu.VMEM((SP, D * K), f32),
            pltpu.VMEM((rows, D * K), jnp.bfloat16),
            pltpu.VMEM((rows, D * K), jnp.bfloat16),
            pltpu.VMEM((ITERS, R, DP, D * K), f32),
            pltpu.VMEM((ITERS, R, DP, D * K), f32),
            pltpu.VMEM((ITERS, R, DP, D * K), f32),
            pltpu.VMEM((ITERS, S, depots, K), f32),
            DMA((moved + 5,)),
            DMA((moved, D)),
            DMA((moved, D)),
            DMA((D, R)),
            DMA((D, R)),
            DMA((ITERS, R)),
            DMA((ITERS, R)),
            DMA((ITERS, R)),
            DMA((ITERS, R)),
            DMA((ITERS, S)),
            DMA((ITERS, S)),
            DMA((3 * ages + 3,)),
            DMA((3 * ages + 3, D)),
            DMA((3 * ages + 3, D)),
            DMA((D, R)),
            DMA((D, R)),
        ],
        compiler_params=pltpu.CompilerParams(collective_id=0, has_side_effects=True),
    )(
        shipments_init.reshape(rows, 1, items),
        holdings_init.reshape(stores, ages, 1, items),
        selling_init.reshape(stores, ages, 1, items),
        shortage_init.reshape(stores, 1, items),
        ordering_init,
        balance_dual_init.reshape(stores, ages, 1, items),
        demand_dual_init.reshape(stores, 1, items),
        depot_dual_init.reshape(depots, 1, items),
        demand_base,
        demand_pattern,
        demand_index.reshape(1, stores),
        jnp.transpose(initial_stock, (1, 0, 2)),
        depot_supply.reshape(depots, 1, items),
        lane_cost,
        item_volume.reshape(1, items),
        holding_cost,
        unit_price.reshape(1, items),
        short_penalty.reshape(1, items),
        order_cost.reshape(1, items),
        lane_depot,
        lane_store,
        lane_mask,
    )
    return (
        outs[0].reshape(shipments_init.shape),
        outs[1].reshape(holdings_init.shape),
        outs[2].reshape(holdings_init.shape),
        outs[3],
        outs[4].reshape(holdings_init.shape),
        outs[5].reshape(depot_dual_init.shape),
    )


def solution(mesh):
    placed = (
        P("scen", "region", None, None, "day", None),
        P("scen", "region", "day", None, None),
        P("scen", "region", "day", None, None),
        P("scen", "region", "day", None),
        P("region", None),
        P("scen", "region", "day", None, None),
        P("scen", "region", "day", None),
        P("scen", "region", "day", None),
        P("region", None),
        P(),
        P("scen", "region", "day"),
        P("region", None, None),
        P("region", "day", None),
        P(),
        P(),
        P(),
        P(),
        P(),
        P(),
        P(),
        P(),
        P(),
    )
    return jax.shard_map(
        functools.partial(
            per_device, mesh.shape["day"], mesh.shape["region"], mesh.shape["scen"]
        ),
        mesh=mesh,
        in_specs=placed,
        out_specs=(
            P("scen", "region", None, None, "day", None),
            P("scen", "region", "day", None, None),
            P("scen", "region", "day", None, None),
            P("region", None),
            P("scen", "region", "day", None, None),
            P("scen", "region", "day", None),
        ),
        check_vma=False,
    )
```
